32 devices in a mesh: row: 4 (over x, core), col: 2 (over y), depth: 4 (over z).
Axes of the slice: x: 2, y: 2, z: 4, core: 2. Of those that a mesh axis runs over, the one named last changes fastest.
Arguments:
- tokens: bfloat16 [2048, 8192], P('col', ('row', 'depth')), may hold values from -6 to 6
- weight: bfloat16 [8192, 24576], P(('row', 'depth'), 'col'), may hold values from -0.0625 to 0.0625
- prev_tokens: bfloat16 [2048, 8192], P('col', ('row', 'depth')), may hold values from -6 to 6
- prev_grad: bfloat16 [2048, 24576], P(('row', 'depth'), 'col'), may hold values from -0.3125 to 0.3125
Outputs:
- qkv: bfloat16 [2048, 24576], P(('row', 'depth'), 'col')
- weight_grad: float32 [8192, 24576], P(('row', 'depth'), 'col')
The draws below stay inside these ranges and needn't reach their ends.
All inputs are finite; a program needn't handle non-finite values.
Results may differ from the reference program's by a relative error of at most 0.001.
Values may be sent and summed in bfloat16 or wider, within the bound.
No kernel may reach another device: no remote copies, remote signals or barrier semaphores. Data moves between devices by JAX's collectives and lax.ppermute only.
A program may use at most 256 MiB of HBM per device.

```python
import jax
import jax.numpy as jnp

D = 8192
TOKENS = 2048


def raised(entries, rng, source, target, blocks, factor):
    owner, partner = [(jnp.arange(entries.shape[position]) // (entries.shape[position] // blocks)).reshape([-1 if axis == position else 1 for axis in range(entries.ndim)]) for position in (source, target)]
    chosen = jax.random.permutation(rng, blocks)[partner]
    strong = (owner == chosen) | (owner == (partner + blocks // 2) % blocks)
    return jnp.where(strong, factor * entries, entries)


def shard_levels(key, shape, split, low, high):
    level, own = 1.0, jax.random.fold_in(key, 6)
    for axis_at, shards_of in split:
        heights = jnp.exp(jax.random.uniform(jax.random.fold_in(own, axis_at), (shards_of,), jnp.float32, low / len(split), high / len(split)))
        level = level * jnp.repeat(heights, shape[axis_at] // shards_of).reshape([-1 if axis == axis_at else 1 for axis in range(len(shape))])
    return level


def bell_draw(key, dims, spread, bound, pieces=(), kind=jnp.bfloat16):
    gain = shard_levels(key, dims, pieces, -0.22, 0.18) if pieces else 1.0
    drawn = jax.random.normal(key, dims, jnp.float32) * spread * gain
    return jnp.minimum(jnp.maximum(drawn, -bound), bound).astype(kind)


def heavy_noise(key, shape, spread, most, split, heavy, held_as=jnp.bfloat16):
    entries = spread * jax.random.normal(key, shape, jnp.float32)
    if split:
        entries = entries * shard_levels(key, shape, split, -0.22, 0.18)
    return jnp.clip(raised(entries, jax.random.fold_in(key, 3), *heavy), -most, most).astype(held_as)


def setup_inputs(seed: int = 0) -> dict:
    arg_keys = jax.random.split(jax.random.key(seed), 5)
    return {
        "tokens": heavy_noise(arg_keys[0], (TOKENS, D), 1.0, 6.0, ((0, 2), (1, 16)), (1, 0, 16, 2.0)),
        "weight": bell_draw(arg_keys[1], (D, 3 * D), D ** -0.5, 0.0625, ((0, 16), (1, 2))),
        "prev_tokens": bell_draw(arg_keys[2], (TOKENS, D), 1.0, 6.0, ((0, 2), (1, 16))),
        "prev_grad": bell_draw(arg_keys[3], (TOKENS, 3 * D), 0.02, 0.3125, ((0, 16), (1, 2))),
    }


def reference(tokens, weight, prev_tokens, prev_grad):
    qkv = jnp.dot(tokens, weight, preferred_element_type=jnp.float32).astype(jnp.bfloat16)
    weight_grad = jnp.dot(prev_tokens.T, prev_grad, preferred_element_type=jnp.float32)
    return qkv, weight_grad
```

```python
import jax
import jax.numpy as jnp
from jax import lax
from jax.sharding import PartitionSpec as P

CORES = 2


def make_local(row_size, chunks):
    high = row_size // CORES

    def moved(shift):
        return [(h * CORES + c, ((h + shift) % high) * CORES + c) for h in range(high) for c in range(CORES)]

    swap = [(h * CORES + c, h * CORES + 1 - c) for h in range(high) for c in range(CORES)]

    def over_chips(block):
        return jnp.concatenate([block] + [lax.ppermute(block, "row", moved(s)) for s in range(1, high)], axis=0)

    def orders():
        r = lax.axis_index("row")
        h, c = r // CORES, r % CORES
        return [[((h + high - s) % high) * CORES + k for s in range(high)] for k in (c, 1 - c)]

    def picked(array, axis, width, order):
        return jnp.concatenate([lax.dynamic_slice_in_dim(array, i * width, width, axis) for i in order], axis=axis)

    def local(tokens, weight, prev_tokens, prev_grad):
        own, other = orders()
        k_width = weight.shape[0]
        step = weight.shape[1] // chunks

        prev_rows = lax.all_gather(prev_grad, "depth", axis=0, tiled=True)
        pieces = [weight[:, i * step:(i + 1) * step] for i in range(chunks)]
        paired = [over_chips(piece) for piece in pieces]

        full = lax.all_gather(tokens, "col", axis=0, tiled=True)
        mine = lax.all_to_all(full, "row", split_axis=0, concat_axis=1, tiled=True)
        t_own = picked(mine, 1, k_width, own)
        t_other = picked(mine, 1, k_width, other)

        summed = []
        for pair in paired:
            across = lax.ppermute(pair, "row", swap)
            partial = jnp.dot(t_own, pair, preferred_element_type=jnp.float32)
            partial = partial + jnp.dot(t_other, across, preferred_element_type=jnp.float32)
            out = lax.psum_scatter(partial, "depth", scatter_dimension=0, tiled=True)
            summed.append(out.astype(jnp.bfloat16))
        qkv = jnp.concatenate(summed, axis=1)

        prev_full = lax.all_gather(prev_tokens, "col", axis=0, tiled=True)
        height = prev_full.shape[0] // row_size
        g_own = over_chips(prev_rows)
        g_other = lax.ppermute(g_own, "row", swap)
        contract = (((0,), (0,)), ((), ()))
        weight_grad = lax.dot_general(
            picked(prev_full, 0, height, own), g_own, contract, preferred_element_type=jnp.float32
        ) + lax.dot_general(
            picked(prev_full, 0, height, other), g_other, contract, preferred_element_type=jnp.float32
        )
        return (qkv, weight_grad)

    return local


def solution(mesh):
    placed = (
        P("col", ("row", "depth")),
        P(("row", "depth"), "col"),
        P("col", ("row", "depth")),
        P(("row", "depth"), "col"),
    )
    return jax.shard_map(
        make_local(mesh.shape["row"], 4),
        mesh=mesh,
        in_specs=placed,
        out_specs=(P(("row", "depth"), "col"), P(("row", "depth"), "col")),
        check_vma=False,
    )
```
